32 devices in a mesh: pair: 16 (over z, x, core), virt: 2 (over y).
Axes of the slice: x: 2, y: 2, z: 4, core: 2. Of those that a mesh axis runs over, the one named last changes fastest.
Arguments:
- amplitudes: bfloat16 [96, 96, 128, 128], P('pair', None, 'virt'), may hold values from -6 to 6
- integrals: bfloat16 [128, 20, 128, 128], P('virt'), may hold values from -0.125 to 0.125
- cd_tiles: int32 [128, 20], P('virt'), may hold values from 0 to 127, as said below
- tile_counts: int32 [128], P('virt'), may hold values from 10 to 20, as said below
- eps_occ: float32 [96], replicated, may hold values from -2 to -0.5
- eps_virt: float32 [128], replicated, may hold values from 0.5 to 3
Outputs:
- new_amplitudes: bfloat16 [96, 96, 128, 128], P('pair', None, 'virt')
The draws below stay inside these ranges and needn't reach their ends.
Inputs may be any that keep to these rules, and one draw needn't show every extreme that they name: `cd_tiles`: row a holds 20 different numbers from lo(a) to lo(a) + 2 * 64 - 1, where lo(a) = min(max(a - 64, 0), 0); only its first tile_counts[a] entries are live. `tile_counts`: some entry equals 20.
All inputs are finite; a program needn't handle non-finite values.
Results may differ from the reference program's by a relative error of at most 0.001.
Values may be sent and summed in bfloat16 or wider, within the bound.
A program may use at most 448 MiB of HBM per device.

```python
import jax
import jax.numpy as jnp
from jax import lax

O = 96
NVW = 128
CAP = 20
A_DEV = 64


def tile_table(key):
    base = jax.random.fold_in(key, 1234)
    first, second, third = jax.random.split(base, 3)
    counts = jax.random.randint(first, (NVW,), CAP - CAP // 2, CAP + 1)
    position = jax.random.randint(second, (), 0, NVW)
    positions = jnp.arange(NVW, dtype=jnp.int32)
    counts = jnp.where(positions == position, CAP, counts).astype(jnp.int32)
    lowest = jnp.clip(positions - A_DEV, 0, NVW - 2 * A_DEV)
    row_keys = jax.random.split(third, NVW)

    def permute_row(row_key):
        return jax.random.permutation(row_key, 2 * A_DEV)
    orders = jax.vmap(permute_row)(row_keys)
    tile_list = lowest[:, None] + orders[:, :CAP]
    return (tile_list.astype(jnp.int32), counts)


def draw_cd_tiles(key, part):
    return tile_table(key)[0]


def draw_tile_counts(key, part):
    return tile_table(key)[1]


def block_levels(stream_key, shape, cuts, low, high):
    factor_of, own = 1.0, jax.random.fold_in(stream_key, 6)
    for dim, blocks in cuts:
        steps = jnp.exp(jax.random.uniform(jax.random.fold_in(own, dim), (blocks,), jnp.float32, low / len(cuts), high / len(cuts)))
        factor_of = factor_of * jnp.repeat(steps, shape[dim] // blocks).reshape([-1 if axis == dim else 1 for axis in range(len(shape))])
    return factor_of


def scatter_about(key, dims, deviation, reach, shards=(), kind=jnp.bfloat16):
    drawn = jax.random.normal(key, dims, jnp.float32) * deviation
    if len(shards) > 0:
        drawn = block_levels(key, dims, shards, -0.22, 0.18) * drawn
    return jnp.clip(drawn, min=-reach, max=reach).astype(kind)


def setup_inputs(seed: int = 0) -> dict:
    streams_of = jax.random.split(jax.random.key(seed), 7)
    return {
        "amplitudes": scatter_about(streams_of[0], (O, O, NVW, NVW), 1.0, 6.0, ((0, 16), (2, 2))),
        "integrals": scatter_about(streams_of[1], (NVW, CAP, NVW, NVW), (CAP * NVW) ** -0.5, 0.125, ((0, 2),)),
        "cd_tiles": draw_cd_tiles(jax.random.fold_in(streams_of[6], 71), 0),
        "tile_counts": draw_tile_counts(jax.random.fold_in(streams_of[6], 71), 0),
        "eps_occ": jnp.clip(jax.random.uniform(streams_of[4], (O,), jnp.float32, -2.0, -0.5), -2.0, -0.5),
        "eps_virt": jnp.clip(jax.random.uniform(streams_of[5], (NVW,), jnp.float32, 0.5, 3.0), 0.5, 3.0),
    }


def reference(amplitudes, integrals, cd_tiles, tile_counts, eps_occ, eps_virt):
    slot_ids = jnp.arange(CAP, dtype=jnp.int32)
    live_slots = (slot_ids[None, :] < tile_counts[:, None]).astype(jnp.float32)

    def one_column(operands):
        tile_list, weights, kept = operands
        picked = jnp.take(amplitudes, tile_list.astype(jnp.int32), axis=2).astype(jnp.float32)
        masked = weights.astype(jnp.float32) * kept[:, None, None]
        return jnp.einsum("ijsd,sdb->ijb", picked, masked)

    ladder = lax.map(one_column, (cd_tiles, integrals, live_slots))
    ladder = jnp.transpose(ladder, (1, 2, 0, 3))
    symmetric = ladder + jnp.transpose(ladder, (1, 0, 3, 2))
    denominator = (eps_occ[:, None, None, None] + eps_occ[None, :, None, None]
                   - eps_virt[None, None, :, None] - eps_virt[None, None, None, :])
    return (symmetric / denominator).astype(jnp.bfloat16)
```

```python
import functools

import jax
import jax.numpy as jnp
from jax import lax
from jax.experimental import pallas as pl
from jax.experimental.pallas import tpu as pltpu
from jax.sharding import PartitionSpec as P

MESH = pl.DeviceIdType.MESH
CHUNKS = 3
GROUP = 4
TOP = 32767.0


def extended(cells, sides, width):
    for axis, dim in sides:
        count = lax.axis_size(axis)
        ends = count - 1
        head = lax.slice_in_dim(cells, 0, width, axis=dim)
        tail = lax.slice_in_dim(cells, cells.shape[dim] - width, cells.shape[dim], axis=dim)
        cells = jnp.concatenate(
            [
                lax.ppermute(tail, axis, [(i, (i + 1) % count) for i in range(ends)]),
                cells,
                lax.ppermute(head, axis, [((i + 1) % count, i) for i in range(ends)]),
            ],
            axis=dim,
        )
    return cells


def general_device(amplitudes, integrals, cd_tiles, tile_counts, eps_occ, eps_virt):
    own_rows = amplitudes.shape[0]
    own_tiles = amplitudes.shape[2]
    slot_count = integrals.shape[1]
    first_tile = lax.axis_index("virt") * own_tiles
    first_row = lax.axis_index("pair") * own_rows
    local_tiles = cd_tiles - first_tile + own_tiles
    slot_ids = lax.broadcasted_iota(jnp.int32, cd_tiles.shape, 1)
    kept_slots = (slot_ids < tile_counts[:, None]).astype(jnp.bfloat16)
    masked_weights = integrals * kept_slots[:, :, None, None]
    padded = extended(amplitudes, (("virt", 2),), own_tiles)
    block_width = min(4, slot_count)
    ladder = None
    for block_start in range(0, slot_count, block_width):
        block_stop = min(block_start + block_width, slot_count)
        columns = local_tiles[:, block_start:block_stop]
        picked = jnp.take(padded, columns, axis=2)
        weights = masked_weights[:, block_start:block_stop]
        term = jnp.einsum("ijasd,asdb->ijab", picked, weights, preferred_element_type=jnp.float32)
        ladder = term if ladder is None else ladder + term
    arrived_ladder = lax.all_to_all(
        lax.all_to_all(ladder, "pair", split_axis=1, concat_axis=0, tiled=True),
        "virt",
        split_axis=3,
        concat_axis=2,
        tiled=True,
    )
    partner = jnp.transpose(arrived_ladder, (1, 0, 3, 2))
    occupied_own = lax.dynamic_slice_in_dim(eps_occ, first_row, own_rows)
    virtual_own = lax.dynamic_slice_in_dim(eps_virt, first_tile, own_tiles)
    denominator = (
        occupied_own[:, None, None, None]
        + eps_occ[None, :, None, None]
        - virtual_own[None, None, :, None]
        - eps_virt[None, None, None, :]
    )
    return ((ladder + partner) / denominator).astype(jnp.bfloat16)


def ladder_kernel(pairs, tiles, loops, own, other, weights, ladder, codes, scales, picked, sems):
    k, h, s = pl.program_id(0), pl.program_id(1), pl.program_id(2)
    steps, halves, eight = pl.num_programs(0), pl.num_programs(1), pl.num_programs(2)
    held = own.shape[0]
    rows, depth = own.shape[1], own.shape[2]
    wide = ladder.shape[3]
    half = wide // 2

    @pl.when((k == 0) & (h == 0) & (s == 0))
    def _():
        first = pltpu.make_async_copy(own, picked.at[pl.ds(0, held)], sems.at[0])
        second = pltpu.make_async_copy(other, picked.at[pl.ds(held, held)], sems.at[1])
        first.start()
        second.start()
        picked[2 * held] = jnp.zeros((rows, depth), picked.dtype)
        first.wait()
        second.wait()

    a = (h * steps + k) * eight + s

    def add(g, total):
        lhs = jnp.concatenate([picked[tiles[a, g * GROUP + x]] for x in range(GROUP)], axis=1)
        rhs = weights[0, pl.ds(g * GROUP, GROUP)].reshape(GROUP * depth, wide)
        return total + jnp.dot(lhs, rhs, preferred_element_type=jnp.float32)

    total = lax.fori_loop(0, loops[a], add, jnp.zeros((rows, wide), jnp.float32))
    ladder[h, 0, pl.ds(s, rows, stride=8), :] = total

    @pl.when((h == halves - 1) & (s == eight - 1))
    def _():
        tall = codes.shape[3]
        low = lax.broadcasted_iota(jnp.int32, (tall, wide), 1) < half

        def largest(p, tops):
            spot = pl.ds(pl.multiple_of(p * tall, 8), tall)
            return tuple(
                jnp.maximum(
                    top,
                    jnp.max(jnp.abs(ladder[x, 0, spot, :]).reshape(tall // 8, 8, wide), axis=0),
                )
                for x, top in enumerate(tops)
            )

        tops = lax.fori_loop(0, pairs, largest, (jnp.zeros((8, wide), jnp.float32),) * 2)
        tops = [jnp.maximum(jnp.max(top, axis=0, keepdims=True), 1e-30) for top in tops]
        sizes = [top / TOP for top in tops]
        factors = [TOP / top for top in tops]
        low_row = low[:1]
        scales[0, pl.ds(k, 1), :] = jnp.where(low_row, sizes[0], pltpu.roll(sizes[1], half, 1))
        scales[1, pl.ds(k, 1), :] = jnp.where(low_row, pltpu.roll(sizes[0], half, 1), sizes[1])

        def pack(p, _):
            spot = pl.ds(pl.multiple_of(p * tall, 8), tall)
            zero, one = (jnp.round(ladder[x, 0, spot, :] * factors[x]) for x in range(2))
            left = jnp.where(low, zero, pltpu.roll(one, half, 1))
            right = jnp.where(low, pltpu.roll(zero, half, 1), one)
            codes[p, 0, 0] = left.astype(jnp.int32).astype(jnp.int16)
            codes[p, 1, 0] = right.astype(jnp.int32).astype(jnp.int16)
            return 0

        lax.fori_loop(0, pairs, pack, 0)


def exchange_kernel(pairs, virts, codes, scales, arrived, sizes, send, recv, send_s, recv_s, own):
    mine_p, mine_v = lax.axis_index("pair"), lax.axis_index("virt")
    me = mine_p * virts + mine_v
    count = pairs * virts
    barrier = pltpu.get_barrier_semaphore()

    def target(d):
        t = lax.rem(me + d, count)
        return t // virts, lax.rem(t, virts)

    def greet(d, _):
        p, v = target(d)
        pl.semaphore_signal(barrier, inc=1, device_id=(p, v), device_id_type=MESH)
        return 0

    lax.fori_loop(1, count, greet, 0)
    keep = pltpu.make_async_copy(codes.at[mine_p, mine_v], arrived.at[mine_p, mine_v], own.at[0])
    keep_s = pltpu.make_async_copy(scales.at[mine_v], sizes.at[mine_p, mine_v], own.at[1])
    keep.start()
    keep_s.start()
    pl.semaphore_wait(barrier, count - 1)

    def copies(d):
        p, v = target(d)
        return (
            pltpu.make_async_remote_copy(
                src_ref=codes.at[p, v],
                dst_ref=arrived.at[mine_p, mine_v],
                send_sem=send.at[d],
                recv_sem=recv.at[d],
                device_id=(p, v),
                device_id_type=MESH,
            ),
            pltpu.make_async_remote_copy(
                src_ref=scales.at[v],
                dst_ref=sizes.at[mine_p, mine_v],
                send_sem=send_s.at[d],
                recv_sem=recv_s.at[d],
                device_id=(p, v),
                device_id_type=MESH,
            ),
        )

    def begin(d, _):
        for copy in copies(d):
            copy.start()
        return 0

    def finish(d, _):
        for copy in copies(d):
            copy.wait()
        return 0

    lax.fori_loop(1, count, begin, 0)
    lax.fori_loop(1, count, finish, 0)
    keep.wait()
    keep_s.wait()


def combine_kernel(chunks, rows, *refs):
    occ_own, occ_all, virt_own, virt_all = refs[:4]
    ladders = refs[4 : 4 + chunks]
    codes = refs[4 + chunks : 4 + 2 * chunks]
    scales = refs[4 + 2 * chunks : 4 + 3 * chunks]
    out = refs[4 + 3 * chunks]
    values = refs[5 + 3 * chunks]
    p = pl.program_id(0)
    virts, steps, tall, wide = codes[0].shape[1:]
    part = rows // chunks
    quarter = steps * 8
    half = wide // 2
    for r in range(chunks):
        for v in range(virts):
            for k in range(steps):
                values[r, v, k] = codes[r][0, v, k].astype(jnp.float32) * scales[r][0, v, k : k + 1, :]
    low = virt_own[...] + virt_all[...]
    for jj in range(rows):
        chunk, inner = jj // part, jj % part
        for i in range(rows):
            spot = pl.ds((inner * rows + i) * 8, 8)
            tile = values[chunk, :, :, spot, :].reshape(virts * quarter, wide)
            turned = tile.T
            partner = jnp.concatenate(
                [
                    turned[x * half : (x + 1) * half, v * quarter : (v + 1) * quarter]
                    for v in range(virts)
                    for x in range(2)
                ],
                axis=1,
            )
            here = pl.ds(((i % part) * rows + jj) * 8, 8)
            mine = ladders[i // part][:, :, 0, here, :].reshape(2 * quarter, wide)
            level = occ_own[i] + occ_all[p * rows + jj]
            out[i, jj] = ((mine + partner) / (level - low)).astype(out.dtype)


def per_device(amplitudes, integrals, cd_tiles, tile_counts, eps_occ, eps_virt):
    pairs, virts = lax.axis_size("pair"), lax.axis_size("virt")
    rows, others, held, depth = amplitudes.shape
    slots, wide = integrals.shape[1], integrals.shape[3]
    fits = virts == 2 and held % 16 == 0 and rows % CHUNKS == 0 and slots % GROUP == 0
    fits = fits and wide == 2 * held and wide == 128 and (rows // CHUNKS * rows) % 2 == 0
    if not fits:
        return general_device(amplitudes, integrals, cd_tiles, tile_counts, eps_occ, eps_virt)
    part = rows // CHUNKS
    block = part * rows
    count = pairs * block
    tall = block * 8
    steps = held // 16
    first_tile = lax.axis_index("virt") * held
    first_row = lax.axis_index("pair") * rows
    slot_ids = lax.broadcasted_iota(jnp.int32, cd_tiles.shape, 1)
    places = lax.rem(cd_tiles - first_tile + 2 * held, 2 * held)
    tiles = jnp.where(slot_ids < tile_counts[:, None], places, 2 * held)
    loops = (tile_counts + GROUP - 1) // GROUP

    ladders, arrived, sizes = [], [], []
    swapped = []
    for r in range(CHUNKS):
        own = amplitudes[r * part : (r + 1) * part].reshape(part, pairs, rows, held, depth)
        own = jnp.transpose(own, (3, 1, 0, 2, 4)).reshape(held, count, depth)
        swapped.append((own, lax.ppermute(own, "virt", [(0, 1), (1, 0)])))
    for r in range(CHUNKS):
        own, other = swapped[r]
        ladder, codes, scale = pl.pallas_call(
            functools.partial(ladder_kernel, pairs),
            grid_spec=pltpu.PrefetchScalarGridSpec(
                num_scalar_prefetch=2,
                grid=(steps, 2, 8),
                in_specs=[
                    pl.BlockSpec(memory_space=pl.ANY),
                    pl.BlockSpec(memory_space=pl.ANY),
                    pl.BlockSpec(
                        (1, slots, depth, wide),
                        lambda k, h, s, *_: ((h * steps + k) * 8 + s, 0, 0, 0),
                    ),
                ],
                out_specs=[
                    pl.BlockSpec((2, 1, count * 8, wide), lambda k, h, s, *_: (0, k, 0, 0)),
                    pl.BlockSpec((pairs, 2, 1, tall, wide), lambda k, h, s, *_: (0, 0, k, 0, 0)),
                    pl.BlockSpec((2, 8, wide), lambda k, h, s, *_: (0, 0, 0)),
                ],
                scratch_shapes=[
                    pltpu.VMEM((2 * held + 1, count, depth), amplitudes.dtype),
                    pltpu.SemaphoreType.DMA((2,)),
                ],
            ),
            out_shape=[
                jax.ShapeDtypeStruct((2, steps, count * 8, wide), jnp.float32),
                jax.ShapeDtypeStruct((pairs, 2, steps, tall, wide), jnp.int16),
                jax.ShapeDtypeStruct((2, 8, wide), jnp.float32),
            ],
            cost_estimate=pl.CostEstimate(
                flops=2 * count * held * slots * depth * wide,
                bytes_accessed=2 * integrals.size,
                transcendentals=0,
            ),
            compiler_params=pltpu.CompilerParams(vmem_limit_bytes=60 * 2**20),
            name=f"ladder_{r}",
        )(tiles, loops, own, other, integrals)
        got, size = pl.pallas_call(
            functools.partial(exchange_kernel, pairs, virts),
            in_specs=[pl.BlockSpec(memory_space=pl.ANY)] * 2,
            out_specs=[pl.BlockSpec(memory_space=pl.ANY)] * 2,
            out_shape=[
                jax.ShapeDtypeStruct(codes.shape, codes.dtype),
                jax.ShapeDtypeStruct((pairs,) + scale.shape, scale.dtype),
            ],
            scratch_shapes=[pltpu.SemaphoreType.DMA((pairs * virts,))] * 4
            + [pltpu.SemaphoreType.DMA((2,))],
            compiler_params=pltpu.CompilerParams(collective_id=r, has_side_effects=True),
            name=f"exchange_{r}",
        )(codes, scale)
        ladders.append(ladder.reshape(2, steps, pairs, tall, wide))
        arrived.append(got)
        sizes.append(size)
    occ_own = lax.dynamic_slice_in_dim(eps_occ, first_row, rows)
    virt_own = lax.dynamic_slice_in_dim(eps_virt, first_tile, held)
    smem = pl.BlockSpec(memory_space=pltpu.SMEM)
    vmem = pl.BlockSpec(memory_space=pltpu.VMEM)
    return pl.pallas_call(
        functools.partial(combine_kernel, CHUNKS, rows),
        grid=(pairs,),
        in_specs=[smem, smem, vmem, vmem]
        + [pl.BlockSpec((2, steps, 1, tall, wide), lambda p: (0, 0, p, 0, 0))] * CHUNKS
        + [pl.BlockSpec((1, 2, steps, tall, wide), lambda p: (p, 0, 0, 0, 0))] * CHUNKS
        + [pl.BlockSpec((1, 2, 8, wide), lambda p: (p, 0, 0, 0))] * CHUNKS,
        out_specs=pl.BlockSpec((rows, rows, held, wide), lambda p: (0, p, 0, 0)),
        out_shape=jax.ShapeDtypeStruct(amplitudes.shape[:3] + (wide,), jnp.bfloat16),
        scratch_shapes=[pltpu.VMEM((CHUNKS, 2, steps, tall, wide), jnp.float32)],
        name="combine",
    )(
        occ_own,
        eps_occ,
        jnp.broadcast_to(virt_own[:, None], (held, wide)),
        jnp.broadcast_to(eps_virt[None, :], (held, wide)),
        *ladders,
        *arrived,
        *sizes,
    )


def solution(mesh):
    in_specs = (
        P("pair", None, "virt", None),
        P("virt", None, None, None),
        P("virt", None),
        P("virt"),
        P(),
        P(),
    )
    out_specs = P("pair", None, "virt", None)
    return jax.shard_map(
        per_device, mesh=mesh, in_specs=in_specs, out_specs=out_specs, check_vma=False
    )
```

```python
import functools

import jax
import jax.numpy as jnp
from jax import lax
from jax.experimental import pallas as pl
from jax.experimental.pallas import tpu as pltpu
from jax.sharding import PartitionSpec as P

MESH = pl.DeviceIdType.MESH
CHUNKS = 3
TOP = 32767.0


def extended(cells, sides, width):
    for axis, dim in sides:
        count = lax.axis_size(axis)
        ends = count - 1
        head = lax.slice_in_dim(cells, 0, width, axis=dim)
        tail = lax.slice_in_dim(cells, cells.shape[dim] - width, cells.shape[dim], axis=dim)
        cells = jnp.concatenate(
            [
                lax.ppermute(tail, axis, [(i, (i + 1) % count) for i in range(ends)]),
                cells,
                lax.ppermute(head, axis, [((i + 1) % count, i) for i in range(ends)]),
            ],
            axis=dim,
        )
    return cells


def general_device(amplitudes, integrals, cd_tiles, tile_counts, eps_occ, eps_virt):
    own_rows = amplitudes.shape[0]
    own_tiles = amplitudes.shape[2]
    slot_count = integrals.shape[1]
    first_tile = lax.axis_index("virt") * own_tiles
    first_row = lax.axis_index("pair") * own_rows
    local_tiles = cd_tiles - first_tile + own_tiles
    slot_ids = lax.broadcasted_iota(jnp.int32, cd_tiles.shape, 1)
    kept_slots = (slot_ids < tile_counts[:, None]).astype(jnp.bfloat16)
    masked_weights = integrals * kept_slots[:, :, None, None]
    padded = extended(amplitudes, (("virt", 2),), own_tiles)
    block_width = min(4, slot_count)
    ladder = None
    for block_start in range(0, slot_count, block_width):
        block_stop = min(block_start + block_width, slot_count)
        columns = local_tiles[:, block_start:block_stop]
        picked = jnp.take(padded, columns, axis=2)
        weights = masked_weights[:, block_start:block_stop]
        term = jnp.einsum("ijasd,asdb->ijab", picked, weights, preferred_element_type=jnp.float32)
        ladder = term if ladder is None else ladder + term
    arrived_ladder = lax.all_to_all(
        lax.all_to_all(ladder, "pair", split_axis=1, concat_axis=0, tiled=True),
        "virt",
        split_axis=3,
        concat_axis=2,
        tiled=True,
    )
    partner = jnp.transpose(arrived_ladder, (1, 0, 3, 2))
    occupied_own = lax.dynamic_slice_in_dim(eps_occ, first_row, own_rows)
    virtual_own = lax.dynamic_slice_in_dim(eps_virt, first_tile, own_tiles)
    denominator = (
        occupied_own[:, None, None, None]
        + eps_occ[None, :, None, None]
        - virtual_own[None, None, :, None]
        - eps_virt[None, None, None, :]
    )
    return ((ladder + partner) / denominator).astype(jnp.bfloat16)


def ladder_kernel(pairs, tiles, own, other, weights, ladder, codes, scales, picked, sems):
    k, h = pl.program_id(0), pl.program_id(1)
    steps, halves = pl.num_programs(0), pl.num_programs(1)
    held = own.shape[0]
    rows, depth = own.shape[1], own.shape[2]
    slots, wide = weights.shape[1], ladder.shape[3]
    half = wide // 2

    @pl.when((k == 0) & (h == 0))
    def _():
        first = pltpu.make_async_copy(own, picked.at[pl.ds(0, held)], sems.at[0])
        second = pltpu.make_async_copy(other, picked.at[pl.ds(held, held)], sems.at[1])
        first.start()
        second.start()
        picked[2 * held] = jnp.zeros((rows, depth), picked.dtype)
        first.wait()
        second.wait()

    for s in range(8):
        a = (h * steps + k) * 8 + s
        lhs = jnp.concatenate([picked[tiles[a, x]] for x in range(slots)], axis=1)
        ladder[h, 0, pl.ds(s, rows, stride=8), :] = jnp.dot(
            lhs, weights[s].reshape(slots * depth, wide), preferred_element_type=jnp.float32
        )

    @pl.when(h == halves - 1)
    def _():
        tall = codes.shape[3]
        low = lax.broadcasted_iota(jnp.int32, (tall, wide), 1) < half

        def largest(p, tops):
            spot = pl.ds(pl.multiple_of(p * tall, 8), tall)
            return tuple(
                jnp.maximum(
                    top,
                    jnp.max(jnp.abs(ladder[x, 0, spot, :]).reshape(tall // 8, 8, wide), axis=0),
                )
                for x, top in enumerate(tops)
            )

        tops = lax.fori_loop(0, pairs, largest, (jnp.zeros((8, wide), jnp.float32),) * 2)
        tops = [jnp.maximum(jnp.max(top, axis=0, keepdims=True), 1e-30) for top in tops]
        sizes = [top / TOP for top in tops]
        factors = [TOP / top for top in tops]
        low_row = low[:1]
        scales[0, pl.ds(k, 1), :] = jnp.where(low_row, sizes[0], pltpu.roll(sizes[1], half, 1))
        scales[1, pl.ds(k, 1), :] = jnp.where(low_row, pltpu.roll(sizes[0], half, 1), sizes[1])

        def pack(p, _):
            spot = pl.ds(pl.multiple_of(p * tall, 8), tall)
            zero, one = (jnp.round(ladder[x, 0, spot, :] * factors[x]) for x in range(2))
            left = jnp.where(low, zero, pltpu.roll(one, half, 1))
            right = jnp.where(low, pltpu.roll(zero, half, 1), one)
            codes[p, 0, 0] = left.astype(jnp.int32).astype(jnp.int16)
            codes[p, 1, 0] = right.astype(jnp.int32).astype(jnp.int16)
            return 0

        lax.fori_loop(0, pairs, pack, 0)


def exchange_kernel(pairs, virts, codes, scales, arrived, sizes, send, recv, send_s, recv_s, own):
    mine_p, mine_v = lax.axis_index("pair"), lax.axis_index("virt")
    me = mine_p * virts + mine_v
    count = pairs * virts
    barrier = pltpu.get_barrier_semaphore()

    def target(d):
        t = lax.rem(me + d, count)
        return t // virts, lax.rem(t, virts)

    def greet(d, _):
        p, v = target(d)
        pl.semaphore_signal(barrier, inc=1, device_id=(p, v), device_id_type=MESH)
        return 0

    lax.fori_loop(1, count, greet, 0)
    keep = pltpu.make_async_copy(codes.at[mine_p, mine_v], arrived.at[mine_p, mine_v], own.at[0])
    keep_s = pltpu.make_async_copy(scales.at[mine_v], sizes.at[mine_p, mine_v], own.at[1])
    keep.start()
    keep_s.start()
    pl.semaphore_wait(barrier, count - 1)

    def copies(d):
        p, v = target(d)
        return (
            pltpu.make_async_remote_copy(
                src_ref=codes.at[p, v],
                dst_ref=arrived.at[mine_p, mine_v],
                send_sem=send.at[d],
                recv_sem=recv.at[d],
                device_id=(p, v),
                device_id_type=MESH,
            ),
            pltpu.make_async_remote_copy(
                src_ref=scales.at[v],
                dst_ref=sizes.at[mine_p, mine_v],
                send_sem=send_s.at[d],
                recv_sem=recv_s.at[d],
                device_id=(p, v),
                device_id_type=MESH,
            ),
        )

    def begin(d, _):
        for copy in copies(d):
            copy.start()
        return 0

    def finish(d, _):
        for copy in copies(d):
            copy.wait()
        return 0

    lax.fori_loop(1, count, begin, 0)
    lax.fori_loop(1, count, finish, 0)
    keep.wait()
    keep_s.wait()


def combine_kernel(chunks, rows, *refs):
    occ_own, occ_all, virt_own, virt_all = refs[:4]
    ladders = refs[4 : 4 + chunks]
    codes = refs[4 + chunks : 4 + 2 * chunks]
    scales = refs[4 + 2 * chunks : 4 + 3 * chunks]
    out = refs[4 + 3 * chunks]
    values = refs[5 + 3 * chunks]
    p = pl.program_id(0)
    virts, steps, tall, wide = codes[0].shape[1:]
    part = rows // chunks
    quarter = steps * 8
    half = wide // 2
    for r in range(chunks):
        for v in range(virts):
            for k in range(steps):
                values[r, v, k] = codes[r][0, v, k].astype(jnp.float32) * scales[r][0, v, k : k + 1, :]
    low = virt_own[...] + virt_all[...]
    for jj in range(rows):
        chunk, inner = jj // part, jj % part
        for i in range(rows):
            spot = pl.ds((inner * rows + i) * 8, 8)
            tile = values[chunk, :, :, spot, :].reshape(virts * quarter, wide)
            turned = tile.T
            partner = jnp.concatenate(
                [
                    turned[x * half : (x + 1) * half, v * quarter : (v + 1) * quarter]
                    for v in range(virts)
                    for x in range(2)
                ],
                axis=1,
            )
            here = pl.ds(((i % part) * rows + jj) * 8, 8)
            mine = ladders[i // part][:, :, 0, here, :].reshape(2 * quarter, wide)
            level = occ_own[i] + occ_all[p * rows + jj]
            out[i, jj] = ((mine + partner) / (level - low)).astype(out.dtype)


def per_device(amplitudes, integrals, cd_tiles, tile_counts, eps_occ, eps_virt):
    pairs, virts = lax.axis_size("pair"), lax.axis_size("virt")
    rows, others, held, depth = amplitudes.shape
    slots, wide = integrals.shape[1], integrals.shape[3]
    fits = virts == 2 and held % 16 == 0 and rows % CHUNKS == 0
    fits = fits and wide == 2 * held and wide == 128 and (rows // CHUNKS * rows) % 2 == 0
    if not fits:
        return general_device(amplitudes, integrals, cd_tiles, tile_counts, eps_occ, eps_virt)
    part = rows // CHUNKS
    block = part * rows
    count = pairs * block
    tall = block * 8
    steps = held // 16
    first_tile = lax.axis_index("virt") * held
    first_row = lax.axis_index("pair") * rows
    slot_ids = lax.broadcasted_iota(jnp.int32, cd_tiles.shape, 1)
    places = lax.rem(cd_tiles - first_tile + 2 * held, 2 * held)
    tiles = jnp.where(slot_ids < tile_counts[:, None], places, 2 * held)

    ladders, arrived, sizes = [], [], []
    swapped = []
    for r in range(CHUNKS):
        own = amplitudes[r * part : (r + 1) * part].reshape(part, pairs, rows, held, depth)
        own = jnp.transpose(own, (3, 1, 0, 2, 4)).reshape(held, count, depth)
        swapped.append((own, lax.ppermute(own, "virt", [(0, 1), (1, 0)])))
    for r in range(CHUNKS):
        own, other = swapped[r]
        ladder, codes, scale = pl.pallas_call(
            functools.partial(ladder_kernel, pairs),
            grid_spec=pltpu.PrefetchScalarGridSpec(
                num_scalar_prefetch=1,
                grid=(steps, 2),
                in_specs=[
                    pl.BlockSpec(memory_space=pl.ANY),
                    pl.BlockSpec(memory_space=pl.ANY),
                    pl.BlockSpec(
                        (8, slots, depth, wide),
                        lambda k, h, *_: (h * steps + k, 0, 0, 0),
                    ),
                ],
                out_specs=[
                    pl.BlockSpec((2, 1, count * 8, wide), lambda k, h, *_: (0, k, 0, 0)),
                    pl.BlockSpec((pairs, 2, 1, tall, wide), lambda k, h, *_: (0, 0, k, 0, 0)),
                    pl.BlockSpec((2, 8, wide), lambda k, h, *_: (0, 0, 0)),
                ],
                scratch_shapes=[
                    pltpu.VMEM((2 * held + 1, count, depth), amplitudes.dtype),
                    pltpu.SemaphoreType.DMA((2,)),
                ],
            ),
            out_shape=[
                jax.ShapeDtypeStruct((2, steps, count * 8, wide), jnp.float32),
                jax.ShapeDtypeStruct((pairs, 2, steps, tall, wide), jnp.int16),
                jax.ShapeDtypeStruct((2, 8, wide), jnp.float32),
            ],
            cost_estimate=pl.CostEstimate(
                flops=2 * count * held * slots * depth * wide,
                bytes_accessed=2 * integrals.size,
                transcendentals=0,
            ),
            compiler_params=pltpu.CompilerParams(vmem_limit_bytes=60 * 2**20),
            name=f"ladder_{r}",
        )(tiles, own, other, integrals)
        got, size = pl.pallas_call(
            functools.partial(exchange_kernel, pairs, virts),
            in_specs=[pl.BlockSpec(memory_space=pl.ANY)] * 2,
            out_specs=[pl.BlockSpec(memory_space=pl.ANY)] * 2,
            out_shape=[
                jax.ShapeDtypeStruct(codes.shape, codes.dtype),
                jax.ShapeDtypeStruct((pairs,) + scale.shape, scale.dtype),
            ],
            scratch_shapes=[pltpu.SemaphoreType.DMA((pairs * virts,))] * 4
            + [pltpu.SemaphoreType.DMA((2,))],
            compiler_params=pltpu.CompilerParams(collective_id=r, has_side_effects=True),
            name=f"exchange_{r}",
        )(codes, scale)
        ladders.append(ladder.reshape(2, steps, pairs, tall, wide))
        arrived.append(got)
        sizes.append(size)
    occ_own = lax.dynamic_slice_in_dim(eps_occ, first_row, rows)
    virt_own = lax.dynamic_slice_in_dim(eps_virt, first_tile, held)
    smem = pl.BlockSpec(memory_space=pltpu.SMEM)
    vmem = pl.BlockSpec(memory_space=pltpu.VMEM)
    return pl.pallas_call(
        functools.partial(combine_kernel, CHUNKS, rows),
        grid=(pairs,),
        in_specs=[smem, smem, vmem, vmem]
        + [pl.BlockSpec((2, steps, 1, tall, wide), lambda p: (0, 0, p, 0, 0))] * CHUNKS
        + [pl.BlockSpec((1, 2, steps, tall, wide), lambda p: (p, 0, 0, 0, 0))] * CHUNKS
        + [pl.BlockSpec((1, 2, 8, wide), lambda p: (p, 0, 0, 0))] * CHUNKS,
        out_specs=pl.BlockSpec((rows, rows, held, wide), lambda p: (0, p, 0, 0)),
        out_shape=jax.ShapeDtypeStruct(amplitudes.shape[:3] + (wide,), jnp.bfloat16),
        scratch_shapes=[pltpu.VMEM((CHUNKS, 2, steps, tall, wide), jnp.float32)],
        name="combine",
    )(
        occ_own,
        eps_occ,
        jnp.broadcast_to(virt_own[:, None], (held, wide)),
        jnp.broadcast_to(eps_virt[None, :], (held, wide)),
        *ladders,
        *arrived,
        *sizes,
    )


def solution(mesh):
    in_specs = (
        P("pair", None, "virt", None),
        P("virt", None, None, None),
        P("virt", None),
        P("virt"),
        P(),
        P(),
    )
    out_specs = P("pair", None, "virt", None)
    return jax.shard_map(
        per_device, mesh=mesh, in_specs=in_specs, out_specs=out_specs, check_vma=False
    )
```

```python
import functools

import jax
import jax.numpy as jnp
from jax import lax
from jax.experimental import pallas as pl
from jax.experimental.pallas import tpu as pltpu
from jax.sharding import PartitionSpec as P

MESH = pl.DeviceIdType.MESH
CHUNKS = 6
TOP = 32767.0


def extended(cells, sides, width):
    for axis, dim in sides:
        count = lax.axis_size(axis)
        ends = count - 1
        head = lax.slice_in_dim(cells, 0, width, axis=dim)
        tail = lax.slice_in_dim(cells, cells.shape[dim] - width, cells.shape[dim], axis=dim)
        cells = jnp.concatenate(
            [
                lax.ppermute(tail, axis, [(i, (i + 1) % count) for i in range(ends)]),
                cells,
                lax.ppermute(head, axis, [((i + 1) % count, i) for i in range(ends)]),
            ],
            axis=dim,
        )
    return cells


def general_device(amplitudes, integrals, cd_tiles, tile_counts, eps_occ, eps_virt):
    own_rows = amplitudes.shape[0]
    own_tiles = amplitudes.shape[2]
    slot_count = integrals.shape[1]
    first_tile = lax.axis_index("virt") * own_tiles
    first_row = lax.axis_index("pair") * own_rows
    local_tiles = cd_tiles - first_tile + own_tiles
    slot_ids = lax.broadcasted_iota(jnp.int32, cd_tiles.shape, 1)
    kept_slots = (slot_ids < tile_counts[:, None]).astype(jnp.bfloat16)
    masked_weights = integrals * kept_slots[:, :, None, None]
    padded = extended(amplitudes, (("virt", 2),), own_tiles)
    block_width = min(4, slot_count)
    ladder = None
    for block_start in range(0, slot_count, block_width):
        block_stop = min(block_start + block_width, slot_count)
        columns = local_tiles[:, block_start:block_stop]
        picked = jnp.take(padded, columns, axis=2)
        weights = masked_weights[:, block_start:block_stop]
        term = jnp.einsum("ijasd,asdb->ijab", picked, weights, preferred_element_type=jnp.float32)
        ladder = term if ladder is None else ladder + term
    arrived_ladder = lax.all_to_all(
        lax.all_to_all(ladder, "pair", split_axis=1, concat_axis=0, tiled=True),
        "virt",
        split_axis=3,
        concat_axis=2,
        tiled=True,
    )
    partner = jnp.transpose(arrived_ladder, (1, 0, 3, 2))
    occupied_own = lax.dynamic_slice_in_dim(eps_occ, first_row, own_rows)
    virtual_own = lax.dynamic_slice_in_dim(eps_virt, first_tile, own_tiles)
    denominator = (
        occupied_own[:, None, None, None]
        + eps_occ[None, :, None, None]
        - virtual_own[None, None, :, None]
        - eps_virt[None, None, None, :]
    )
    return ((ladder + partner) / denominator).astype(jnp.bfloat16)


def ladder_kernel(pairs, tiles, own, other, weights, ladder, codes, scales, picked, sems):
    k, h = pl.program_id(0), pl.program_id(1)
    steps, halves = pl.num_programs(0), pl.num_programs(1)
    held = own.shape[0]
    rows, depth = own.shape[1], own.shape[2]
    slots, wide = weights.shape[1], ladder.shape[3]
    half = wide // 2

    @pl.when((k == 0) & (h == 0))
    def _():
        first = pltpu.make_async_copy(own, picked.at[pl.ds(0, held)], sems.at[0])
        second = pltpu.make_async_copy(other, picked.at[pl.ds(held, held)], sems.at[1])
        first.start()
        second.start()
        picked[2 * held] = jnp.zeros((rows, depth), picked.dtype)
        first.wait()
        second.wait()

    for s in range(8):
        a = (h * steps + k) * 8 + s
        lhs = jnp.concatenate([picked[tiles[a, x]] for x in range(slots)], axis=1)
        ladder[h, 0, pl.ds(s, rows, stride=8), :] = jnp.dot(
            lhs, weights[s].reshape(slots * depth, wide), preferred_element_type=jnp.float32
        )

    @pl.when(h == halves - 1)
    def _():
        tall = codes.shape[3]
        low = lax.broadcasted_iota(jnp.int32, (tall, wide), 1) < half

        def largest(p, tops):
            spot = pl.ds(pl.multiple_of(p * tall, 8), tall)
            return tuple(
                jnp.maximum(
                    top,
                    jnp.max(jnp.abs(ladder[x, 0, spot, :]).reshape(tall // 8, 8, wide), axis=0),
                )
                for x, top in enumerate(tops)
            )

        tops = lax.fori_loop(0, pairs, largest, (jnp.zeros((8, wide), jnp.float32),) * 2)
        tops = [jnp.maximum(jnp.max(top, axis=0, keepdims=True), 1e-30) for top in tops]
        sizes = [top / TOP for top in tops]
        factors = [TOP / top for top in tops]
        low_row = low[:1]
        scales[0, pl.ds(k, 1), :] = jnp.where(low_row, sizes[0], pltpu.roll(sizes[1], half, 1))
        scales[1, pl.ds(k, 1), :] = jnp.where(low_row, pltpu.roll(sizes[0], half, 1), sizes[1])

        def pack(p, _):
            spot = pl.ds(pl.multiple_of(p * tall, 8), tall)
            zero, one = (jnp.round(ladder[x, 0, spot, :] * factors[x]) for x in range(2))
            left = jnp.where(low, zero, pltpu.roll(one, half, 1))
            right = jnp.where(low, pltpu.roll(zero, half, 1), one)
            codes[p, 0, 0] = left.astype(jnp.int32).astype(jnp.int16)
            codes[p, 1, 0] = right.astype(jnp.int32).astype(jnp.int16)
            return 0

        lax.fori_loop(0, pairs, pack, 0)


class Exchange:
    def __init__(self, pairs, virts, codes, scales, arrived, sizes, send, recv, send_s, recv_s, own):
        self.refs = codes, scales, arrived, sizes, send, recv, send_s, recv_s
        self.virts, self.count = virts, pairs * virts
        self.here = lax.axis_index("pair"), lax.axis_index("virt")
        p, v = self.here
        self.me = p * virts + v
        self.kept = (
            pltpu.make_async_copy(codes.at[p, v], arrived.at[p, v], own.at[0]),
            pltpu.make_async_copy(scales.at[v], sizes.at[p, v], own.at[1]),
        )

    def target(self, d):
        t = lax.rem(self.me + d, self.count)
        return t // self.virts, lax.rem(t, self.virts)

    def copies(self, d):
        codes, scales, arrived, sizes, send, recv, send_s, recv_s = self.refs
        p, v = self.target(d)
        return (
            pltpu.make_async_remote_copy(
                src_ref=codes.at[p, v],
                dst_ref=arrived.at[self.here],
                send_sem=send.at[d],
                recv_sem=recv.at[d],
                device_id=(p, v),
                device_id_type=MESH,
            ),
            pltpu.make_async_remote_copy(
                src_ref=scales.at[v],
                dst_ref=sizes.at[self.here],
                send_sem=send_s.at[d],
                recv_sem=recv_s.at[d],
                device_id=(p, v),
                device_id_type=MESH,
            ),
        )

    def start(self):
        barrier = pltpu.get_barrier_semaphore()

        def greet(d, _):
            pl.semaphore_signal(barrier, inc=1, device_id=self.target(d), device_id_type=MESH)
            return 0

        def begin(d, _):
            for copy in self.copies(d):
                copy.start()
            return 0

        lax.fori_loop(1, self.count, greet, 0)
        pl.semaphore_wait(barrier, self.count - 1)
        lax.fori_loop(1, self.count, begin, 0)
        for copy in self.kept:
            copy.start()

    def wait(self):
        def finish(d, _):
            for copy in self.copies(d):
                copy.wait()
            return 0

        lax.fori_loop(1, self.count, finish, 0)
        for copy in self.kept:
            copy.wait()


def exchange_kernel(pairs, virts, *refs):
    moved = Exchange(pairs, virts, *refs)
    moved.start()
    moved.wait()


def both_kernel(pairs, virts, tiles, own, other, weights, old_codes, old_scales, *refs):
    ladder, codes, scales, arrived, sizes, picked, sems = refs[:7]
    moved = Exchange(pairs, virts, old_codes, old_scales, arrived, sizes, *refs[7:])
    k, h = pl.program_id(0), pl.program_id(1)

    @pl.when((k == 0) & (h == 0))
    def _():
        moved.start()

    ladder_kernel(pairs, tiles, own, other, weights, ladder, codes, scales, picked, sems)

    @pl.when((k == pl.num_programs(0) - 1) & (h == pl.num_programs(1) - 1))
    def _():
        moved.wait()


def combine_kernel(chunks, rows, *refs):
    occ_own, occ_all, virt_own, virt_all = refs[:4]
    ladders = refs[4 : 4 + chunks]
    codes = refs[4 + chunks : 4 + 2 * chunks]
    scales = refs[4 + 2 * chunks : 4 + 3 * chunks]
    out = refs[4 + 3 * chunks]
    values = refs[5 + 3 * chunks]
    p = pl.program_id(0)
    virts, steps, tall, wide = codes[0].shape[1:]
    part = rows // chunks
    quarter = steps * 8
    half = wide // 2
    for r in range(chunks):
        for v in range(virts):
            for k in range(steps):
                values[r, v, k] = codes[r][0, v, k].astype(jnp.float32) * scales[r][0, v, k : k + 1, :]
    low = virt_own[...] + virt_all[...]
    for jj in range(rows):
        chunk, inner = jj // part, jj % part
        for i in range(rows):
            spot = pl.ds((inner * rows + i) * 8, 8)
            tile = values[chunk, :, :, spot, :].reshape(virts * quarter, wide)
            turned = tile.T
            partner = jnp.concatenate(
                [
                    turned[x * half : (x + 1) * half, v * quarter : (v + 1) * quarter]
                    for v in range(virts)
                    for x in range(2)
                ],
                axis=1,
            )
            here = pl.ds(((i % part) * rows + jj) * 8, 8)
            mine = ladders[i // part][:, :, 0, here, :].reshape(2 * quarter, wide)
            level = occ_own[i] + occ_all[p * rows + jj]
            out[i, jj] = ((mine + partner) / (level - low)).astype(out.dtype)


def per_device(amplitudes, integrals, cd_tiles, tile_counts, eps_occ, eps_virt):
    pairs, virts = lax.axis_size("pair"), lax.axis_size("virt")
    rows, others, held, depth = amplitudes.shape
    slots, wide = integrals.shape[1], integrals.shape[3]
    fits = virts == 2 and held % 16 == 0 and rows % CHUNKS == 0
    fits = fits and wide == 2 * held and wide == 128 and (rows // CHUNKS * rows) % 2 == 0
    if not fits:
        return general_device(amplitudes, integrals, cd_tiles, tile_counts, eps_occ, eps_virt)
    part = rows // CHUNKS
    block = part * rows
    count = pairs * block
    tall = block * 8
    steps = held // 16
    first_tile = lax.axis_index("virt") * held
    first_row = lax.axis_index("pair") * rows
    slot_ids = lax.broadcasted_iota(jnp.int32, cd_tiles.shape, 1)
    places = lax.rem(cd_tiles - first_tile + 2 * held, 2 * held)
    tiles = jnp.where(slot_ids < tile_counts[:, None], places, 2 * held)

    ladders, arrived, sizes = [], [], []
    swapped = []
    for r in range(CHUNKS):
        own = amplitudes[r * part : (r + 1) * part].reshape(part, pairs, rows, held, depth)
        own = jnp.transpose(own, (3, 1, 0, 2, 4)).reshape(held, count, depth)
        swapped.append((own, lax.ppermute(own, "virt", [(0, 1), (1, 0)])))
    anywhere = pl.BlockSpec(memory_space=pl.ANY)
    moved_sems = [pltpu.SemaphoreType.DMA((pairs * virts,))] * 4 + [pltpu.SemaphoreType.DMA((2,))]
    moved_shape = [
        jax.ShapeDtypeStruct((pairs, 2, steps, tall, wide), jnp.int16),
        jax.ShapeDtypeStruct((pairs, 2, 8, wide), jnp.float32),
    ]
    last = ()
    for r in range(CHUNKS):
        own, other = swapped[r]
        beside = len(last) > 0
        kernel = functools.partial(both_kernel, pairs, virts)
        extra = {"collective_id": r, "has_side_effects": True} if beside else {}
        ladder, *made = pl.pallas_call(
            kernel if beside else functools.partial(ladder_kernel, pairs),
            grid_spec=pltpu.PrefetchScalarGridSpec(
                num_scalar_prefetch=1,
                grid=(steps, 2),
                in_specs=[
                    anywhere,
                    anywhere,
                    pl.BlockSpec(
                        (8, slots, depth, wide), lambda k, h, *_: (h * steps + k, 0, 0, 0)
                    ),
                ]
                + [anywhere] * len(last),
                out_specs=[
                    pl.BlockSpec((2, 1, count * 8, wide), lambda k, h, *_: (0, k, 0, 0)),
                    pl.BlockSpec((pairs, 2, 1, tall, wide), lambda k, h, *_: (0, 0, k, 0, 0)),
                    pl.BlockSpec((2, 8, wide), lambda k, h, *_: (0, 0, 0)),
                ]
                + [anywhere] * len(last),
                scratch_shapes=[
                    pltpu.VMEM((2 * held + 1, count, depth), amplitudes.dtype),
                    pltpu.SemaphoreType.DMA((2,)),
                ]
                + moved_sems * beside,
            ),
            out_shape=[
                jax.ShapeDtypeStruct((2, steps, count * 8, wide), jnp.float32),
                jax.ShapeDtypeStruct((pairs, 2, steps, tall, wide), jnp.int16),
                jax.ShapeDtypeStruct((2, 8, wide), jnp.float32),
            ]
            + moved_shape * beside,
            cost_estimate=pl.CostEstimate(
                flops=2 * count * held * slots * depth * wide,
                bytes_accessed=2 * integrals.size,
                transcendentals=0,
            ),
            compiler_params=pltpu.CompilerParams(vmem_limit_bytes=60 * 2**20, **extra),
            name=f"ladder_{r}",
        )(tiles, own, other, integrals, *last)
        last = tuple(made[:2])
        ladders.append(ladder.reshape(2, steps, pairs, tall, wide))
        if beside:
            arrived.append(made[2])
            sizes.append(made[3])
    got, size = pl.pallas_call(
        functools.partial(exchange_kernel, pairs, virts),
        in_specs=[anywhere] * 2,
        out_specs=[anywhere] * 2,
        out_shape=moved_shape,
        scratch_shapes=moved_sems,
        compiler_params=pltpu.CompilerParams(collective_id=CHUNKS, has_side_effects=True),
        name="exchange",
    )(*last)
    arrived.append(got)
    sizes.append(size)
    occ_own = lax.dynamic_slice_in_dim(eps_occ, first_row, rows)
    virt_own = lax.dynamic_slice_in_dim(eps_virt, first_tile, held)
    smem = pl.BlockSpec(memory_space=pltpu.SMEM)
    vmem = pl.BlockSpec(memory_space=pltpu.VMEM)
    return pl.pallas_call(
        functools.partial(combine_kernel, CHUNKS, rows),
        grid=(pairs,),
        in_specs=[smem, smem, vmem, vmem]
        + [pl.BlockSpec((2, steps, 1, tall, wide), lambda p: (0, 0, p, 0, 0))] * CHUNKS
        + [pl.BlockSpec((1, 2, steps, tall, wide), lambda p: (p, 0, 0, 0, 0))] * CHUNKS
        + [pl.BlockSpec((1, 2, 8, wide), lambda p: (p, 0, 0, 0))] * CHUNKS,
        out_specs=pl.BlockSpec((rows, rows, held, wide), lambda p: (0, p, 0, 0)),
        out_shape=jax.ShapeDtypeStruct(amplitudes.shape[:3] + (wide,), jnp.bfloat16),
        scratch_shapes=[pltpu.VMEM((CHUNKS, 2, steps, tall, wide), jnp.float32)],
        name="combine",
    )(
        occ_own,
        eps_occ,
        jnp.broadcast_to(virt_own[:, None], (held, wide)),
        jnp.broadcast_to(eps_virt[None, :], (held, wide)),
        *ladders,
        *arrived,
        *sizes,
    )


def solution(mesh):
    in_specs = (
        P("pair", None, "virt", None),
        P("virt", None, None, None),
        P("virt", None),
        P("virt"),
        P(),
        P(),
    )
    out_specs = P("pair", None, "virt", None)
    return jax.shard_map(
        per_device, mesh=mesh, in_specs=in_specs, out_specs=out_specs, check_vma=False
    )
```

```python
import functools

import jax
import jax.numpy as jnp
from jax import lax
from jax.experimental import pallas as pl
from jax.experimental.pallas import tpu as pltpu
from jax.sharding import PartitionSpec as P

MESH = pl.DeviceIdType.MESH
CHUNKS = 6
TOP = 32767.0


def extended(cells, sides, width):
    for axis, dim in sides:
        count = lax.axis_size(axis)
        ends = count - 1
        head = lax.slice_in_dim(cells, 0, width, axis=dim)
        tail = lax.slice_in_dim(cells, cells.shape[dim] - width, cells.shape[dim], axis=dim)
        cells = jnp.concatenate(
            [
                lax.ppermute(tail, axis, [(i, (i + 1) % count) for i in range(ends)]),
                cells,
                lax.ppermute(head, axis, [((i + 1) % count, i) for i in range(ends)]),
            ],
            axis=dim,
        )
    return cells


def general_device(amplitudes, integrals, cd_tiles, tile_counts, eps_occ, eps_virt):
    own_rows = amplitudes.shape[0]
    own_tiles = amplitudes.shape[2]
    slot_count = integrals.shape[1]
    first_tile = lax.axis_index("virt") * own_tiles
    first_row = lax.axis_index("pair") * own_rows
    local_tiles = cd_tiles - first_tile + own_tiles
    slot_ids = lax.broadcasted_iota(jnp.int32, cd_tiles.shape, 1)
    kept_slots = (slot_ids < tile_counts[:, None]).astype(jnp.bfloat16)
    masked_weights = integrals * kept_slots[:, :, None, None]
    padded = extended(amplitudes, (("virt", 2),), own_tiles)
    block_width = min(4, slot_count)
    ladder = None
    for block_start in range(0, slot_count, block_width):
        block_stop = min(block_start + block_width, slot_count)
        columns = local_tiles[:, block_start:block_stop]
        picked = jnp.take(padded, columns, axis=2)
        weights = masked_weights[:, block_start:block_stop]
        term = jnp.einsum("ijasd,asdb->ijab", picked, weights, preferred_element_type=jnp.float32)
        ladder = term if ladder is None else ladder + term
    arrived_ladder = lax.all_to_all(
        lax.all_to_all(ladder, "pair", split_axis=1, concat_axis=0, tiled=True),
        "virt",
        split_axis=3,
        concat_axis=2,
        tiled=True,
    )
    partner = jnp.transpose(arrived_ladder, (1, 0, 3, 2))
    occupied_own = lax.dynamic_slice_in_dim(eps_occ, first_row, own_rows)
    virtual_own = lax.dynamic_slice_in_dim(eps_virt, first_tile, own_tiles)
    denominator = (
        occupied_own[:, None, None, None]
        + eps_occ[None, :, None, None]
        - virtual_own[None, None, :, None]
        - eps_virt[None, None, None, :]
    )
    return ((ladder + partner) / denominator).astype(jnp.bfloat16)


def ladder_kernel(pairs, tiles, own, other, weights, ladder, codes, scales, picked, sems):
    k, h = pl.program_id(0), pl.program_id(1)
    steps, halves = pl.num_programs(0), pl.num_programs(1)
    held = own.shape[0]
    rows, depth = own.shape[1], own.shape[2]
    slots, wide = weights.shape[1], ladder.shape[3]
    half = wide // 2

    @pl.when((k == 0) & (h == 0))
    def _():
        first = pltpu.make_async_copy(own, picked.at[pl.ds(0, held)], sems.at[0])
        second = pltpu.make_async_copy(other, picked.at[pl.ds(held, held)], sems.at[1])
        first.start()
        second.start()
        picked[2 * held] = jnp.zeros((rows, depth), picked.dtype)
        first.wait()
        second.wait()

    for s in range(8):
        a = (h * steps + k) * 8 + s
        lhs = jnp.concatenate([picked[tiles[a, x]] for x in range(slots)], axis=1)
        ladder[h, 0, pl.ds(s, rows, stride=8), :] = jnp.dot(
            lhs, weights[s].reshape(slots * depth, wide), preferred_element_type=jnp.float32
        )

    @pl.when(h == halves - 1)
    def _():
        tall = codes.shape[3]
        low = lax.broadcasted_iota(jnp.int32, (tall, wide), 1) < half

        def largest(p, tops):
            spot = pl.ds(pl.multiple_of(p * tall, 8), tall)
            return tuple(
                jnp.maximum(
                    top,
                    jnp.max(jnp.abs(ladder[x, 0, spot, :]).reshape(tall // 8, 8, wide), axis=0),
                )
                for x, top in enumerate(tops)
            )

        tops = lax.fori_loop(0, pairs, largest, (jnp.zeros((8, wide), jnp.float32),) * 2)
        tops = [jnp.maximum(jnp.max(top, axis=0, keepdims=True), 1e-30) for top in tops]
        sizes = [top / TOP for top in tops]
        factors = [TOP / top for top in tops]
        low_row = low[:1]
        scales[0, pl.ds(k, 1), :] = jnp.where(low_row, sizes[0], pltpu.roll(sizes[1], half, 1))
        scales[1, pl.ds(k, 1), :] = jnp.where(low_row, pltpu.roll(sizes[0], half, 1), sizes[1])

        def pack(p, _):
            spot = pl.ds(pl.multiple_of(p * tall, 8), tall)
            zero, one = (jnp.round(ladder[x, 0, spot, :] * factors[x]) for x in range(2))
            left = jnp.where(low, zero, pltpu.roll(one, half, 1))
            right = jnp.where(low, pltpu.roll(zero, half, 1), one)
            codes[p, 0, 0] = left.astype(jnp.int32).astype(jnp.int16)
            codes[p, 1, 0] = right.astype(jnp.int32).astype(jnp.int16)
            return 0

        lax.fori_loop(0, pairs, pack, 0)


class Exchange:
    def __init__(self, pairs, virts, codes, scales, arrived, sizes, send, recv, send_s, recv_s, own):
        self.refs = codes, scales, arrived, sizes, send, recv, send_s, recv_s
        self.virts, self.count = virts, pairs * virts
        self.here = lax.axis_index("pair"), lax.axis_index("virt")
        p, v = self.here
        self.me = p * virts + v
        self.kept = (
            pltpu.make_async_copy(codes.at[p, v], arrived.at[p, v], own.at[0]),
            pltpu.make_async_copy(scales.at[v], sizes.at[p, v], own.at[1]),
        )

    def target(self, d):
        t = lax.rem(self.me + d, self.count)
        return t // self.virts, lax.rem(t, self.virts)

    def copies(self, d):
        codes, scales, arrived, sizes, send, recv, send_s, recv_s = self.refs
        p, v = self.target(d)
        return (
            pltpu.make_async_remote_copy(
                src_ref=codes.at[p, v],
                dst_ref=arrived.at[self.here],
                send_sem=send.at[d],
                recv_sem=recv.at[d],
                device_id=(p, v),
                device_id_type=MESH,
            ),
            pltpu.make_async_remote_copy(
                src_ref=scales.at[v],
                dst_ref=sizes.at[self.here],
                send_sem=send_s.at[d],
                recv_sem=recv_s.at[d],
                device_id=(p, v),
                device_id_type=MESH,
            ),
        )

    def start(self):
        def begin(d, _):
            for copy in self.copies(d):
                copy.start()
            return 0

        lax.fori_loop(1, self.count, begin, 0)
        for copy in self.kept:
            copy.start()

    def wait(self):
        def finish(d, _):
            for copy in self.copies(d):
                copy.wait()
            return 0

        lax.fori_loop(1, self.count, finish, 0)
        for copy in self.kept:
            copy.wait()


def greet_all(pairs, virts):
    count = pairs * virts
    me = lax.axis_index("pair") * virts + lax.axis_index("virt")
    barrier = pltpu.get_barrier_semaphore()

    def greet(d, _):
        t = lax.rem(me + d, count)
        pl.semaphore_signal(
            barrier, inc=1, device_id=(t // virts, lax.rem(t, virts)), device_id_type=MESH
        )
        return 0

    lax.fori_loop(1, count, greet, 0)
    pl.semaphore_wait(barrier, count - 1)


def exchange_kernel(pairs, virts, *refs):
    moved = Exchange(pairs, virts, *refs)
    greet_all(pairs, virts)
    moved.start()
    moved.wait()


def both_kernel(pairs, virts, beside, more, tiles, own, other, weights, *refs):
    refs = list(refs)
    old = [refs.pop(0) for _ in range(2 * beside)]
    ahead = [refs.pop(0) for _ in range(more)]
    ladder, codes, scales = [refs.pop(0) for _ in range(3)]
    old += [refs.pop(0) for _ in range(2 * beside)]
    ahead += [refs.pop(0) for _ in range(more)]
    picked, sems = refs.pop(0), refs.pop(0)
    tasks = []
    if beside:
        tasks.append(Exchange(pairs, virts, *old, *[refs.pop(0) for _ in range(5)]))
    if more:
        swap_sems = refs.pop(0)
        tasks.append(
            pltpu.make_async_remote_copy(
                src_ref=ahead[0],
                dst_ref=ahead[1],
                send_sem=swap_sems.at[0],
                recv_sem=swap_sems.at[1],
                device_id=(lax.axis_index("pair"), 1 - lax.axis_index("virt")),
                device_id_type=MESH,
            )
        )
    k, h = pl.program_id(0), pl.program_id(1)

    @pl.when((k == 0) & (h == 0))
    def _():
        greet_all(pairs, virts)
        for task in tasks:
            task.start()

    ladder_kernel(pairs, tiles, own, other, weights, ladder, codes, scales, picked, sems)

    @pl.when((k == pl.num_programs(0) - 1) & (h == pl.num_programs(1) - 1))
    def _():
        for task in tasks:
            task.wait()


def combine_kernel(chunks, rows, *refs):
    occ_own, occ_all, virt_own, virt_all = refs[:4]
    ladders = refs[4 : 4 + chunks]
    codes = refs[4 + chunks : 4 + 2 * chunks]
    scales = refs[4 + 2 * chunks : 4 + 3 * chunks]
    out = refs[4 + 3 * chunks]
    values = refs[5 + 3 * chunks]
    p = pl.program_id(0)
    virts, steps, tall, wide = codes[0].shape[1:]
    part = rows // chunks
    quarter = steps * 8
    half = wide // 2
    for r in range(chunks):
        for v in range(virts):
            for k in range(steps):
                values[r, v, k] = codes[r][0, v, k].astype(jnp.float32) * scales[r][0, v, k : k + 1, :]
    low = virt_own[...] + virt_all[...]
    for jj in range(rows):
        chunk, inner = jj // part, jj % part
        for i in range(rows):
            spot = pl.ds((inner * rows + i) * 8, 8)
            tile = values[chunk, :, :, spot, :].reshape(virts * quarter, wide)
            turned = tile.T
            partner = jnp.concatenate(
                [
                    turned[x * half : (x + 1) * half, v * quarter : (v + 1) * quarter]
                    for v in range(virts)
                    for x in range(2)
                ],
                axis=1,
            )
            here = pl.ds(((i % part) * rows + jj) * 8, 8)
            mine = ladders[i // part][:, :, 0, here, :].reshape(2 * quarter, wide)
            level = occ_own[i] + occ_all[p * rows + jj]
            out[i, jj] = ((mine + partner) / (level - low)).astype(out.dtype)


def per_device(amplitudes, integrals, cd_tiles, tile_counts, eps_occ, eps_virt):
    pairs, virts = lax.axis_size("pair"), lax.axis_size("virt")
    rows, others, held, depth = amplitudes.shape
    slots, wide = integrals.shape[1], integrals.shape[3]
    fits = virts == 2 and held % 16 == 0 and rows % CHUNKS == 0
    fits = fits and wide == 2 * held and wide == 128 and (rows // CHUNKS * rows) % 2 == 0
    if not fits:
        return general_device(amplitudes, integrals, cd_tiles, tile_counts, eps_occ, eps_virt)
    part = rows // CHUNKS
    block = part * rows
    count = pairs * block
    tall = block * 8
    steps = held // 16
    first_tile = lax.axis_index("virt") * held
    first_row = lax.axis_index("pair") * rows
    slot_ids = lax.broadcasted_iota(jnp.int32, cd_tiles.shape, 1)
    places = lax.rem(cd_tiles - first_tile + 2 * held, 2 * held)
    tiles = jnp.where(slot_ids < tile_counts[:, None], places, 2 * held)

    ladders, arrived, sizes = [], [], []
    swapped = []
    for r in range(CHUNKS):
        own = amplitudes[r * part : (r + 1) * part].reshape(part, pairs, rows, held, depth)
        own = jnp.transpose(own, (3, 1, 0, 2, 4)).reshape(held, count, depth)
        swapped.append(own)
    other = lax.ppermute(swapped[0], "virt", [(0, 1), (1, 0)])
    anywhere = pl.BlockSpec(memory_space=pl.ANY)
    moved_sems = [pltpu.SemaphoreType.DMA((pairs * virts,))] * 4 + [pltpu.SemaphoreType.DMA((2,))]
    moved_shape = [
        jax.ShapeDtypeStruct((pairs, 2, steps, tall, wide), jnp.int16),
        jax.ShapeDtypeStruct((pairs, 2, 8, wide), jnp.float32),
    ]
    last = ()
    for r in range(CHUNKS):
        own = swapped[r]
        beside = len(last) > 0
        ahead = swapped[r + 1 : r + 2]
        more = len(ahead)
        ladder, *made = pl.pallas_call(
            functools.partial(both_kernel, pairs, virts, beside, more),
            grid_spec=pltpu.PrefetchScalarGridSpec(
                num_scalar_prefetch=1,
                grid=(steps, 2),
                in_specs=[
                    anywhere,
                    anywhere,
                    pl.BlockSpec(
                        (8, slots, depth, wide), lambda k, h, *_: (h * steps + k, 0, 0, 0)
                    ),
                ]
                + [anywhere] * (len(last) + more),
                out_specs=[
                    pl.BlockSpec((2, 1, count * 8, wide), lambda k, h, *_: (0, k, 0, 0)),
                    pl.BlockSpec((pairs, 2, 1, tall, wide), lambda k, h, *_: (0, 0, k, 0, 0)),
                    pl.BlockSpec((2, 8, wide), lambda k, h, *_: (0, 0, 0)),
                ]
                + [anywhere] * (len(last) + more),
                scratch_shapes=[
                    pltpu.VMEM((2 * held + 1, count, depth), amplitudes.dtype),
                    pltpu.SemaphoreType.DMA((2,)),
                ]
                + moved_sems * beside
                + [pltpu.SemaphoreType.DMA((2,))] * more,
            ),
            out_shape=[
                jax.ShapeDtypeStruct((2, steps, count * 8, wide), jnp.float32),
                jax.ShapeDtypeStruct((pairs, 2, steps, tall, wide), jnp.int16),
                jax.ShapeDtypeStruct((2, 8, wide), jnp.float32),
            ]
            + moved_shape * beside
            + [jax.ShapeDtypeStruct(own.shape, own.dtype)] * more,
            cost_estimate=pl.CostEstimate(
                flops=2 * count * held * slots * depth * wide,
                bytes_accessed=2 * integrals.size,
                transcendentals=0,
            ),
            compiler_params=pltpu.CompilerParams(
                vmem_limit_bytes=60 * 2**20, collective_id=r, has_side_effects=True
            ),
            name=f"ladder_{r}",
        )(tiles, own, other, integrals, *last, *ahead)
        last = tuple(made[:2])
        ladders.append(ladder.reshape(2, steps, pairs, tall, wide))
        if beside:
            arrived.append(made[2])
            sizes.append(made[3])
        other = made[-1]
    got, size = pl.pallas_call(
        functools.partial(exchange_kernel, pairs, virts),
        in_specs=[anywhere] * 2,
        out_specs=[anywhere] * 2,
        out_shape=moved_shape,
        scratch_shapes=moved_sems,
        compiler_params=pltpu.CompilerParams(collective_id=CHUNKS, has_side_effects=True),
        name="exchange",
    )(*last)
    arrived.append(got)
    sizes.append(size)
    occ_own = lax.dynamic_slice_in_dim(eps_occ, first_row, rows)
    virt_own = lax.dynamic_slice_in_dim(eps_virt, first_tile, held)
    smem = pl.BlockSpec(memory_space=pltpu.SMEM)
    vmem = pl.BlockSpec(memory_space=pltpu.VMEM)
    return pl.pallas_call(
        functools.partial(combine_kernel, CHUNKS, rows),
        grid=(pairs,),
        in_specs=[smem, smem, vmem, vmem]
        + [pl.BlockSpec((2, steps, 1, tall, wide), lambda p: (0, 0, p, 0, 0))] * CHUNKS
        + [pl.BlockSpec((1, 2, steps, tall, wide), lambda p: (p, 0, 0, 0, 0))] * CHUNKS
        + [pl.BlockSpec((1, 2, 8, wide), lambda p: (p, 0, 0, 0))] * CHUNKS,
        out_specs=pl.BlockSpec((rows, rows, held, wide), lambda p: (0, p, 0, 0)),
        out_shape=jax.ShapeDtypeStruct(amplitudes.shape[:3] + (wide,), jnp.bfloat16),
        scratch_shapes=[pltpu.VMEM((CHUNKS, 2, steps, tall, wide), jnp.float32)],
        name="combine",
    )(
        occ_own,
        eps_occ,
        jnp.broadcast_to(virt_own[:, None], (held, wide)),
        jnp.broadcast_to(eps_virt[None, :], (held, wide)),
        *ladders,
        *arrived,
        *sizes,
    )


def solution(mesh):
    in_specs = (
        P("pair", None, "virt", None),
        P("virt", None, None, None),
        P("virt", None),
        P("virt"),
        P(),
        P(),
    )
    out_specs = P("pair", None, "virt", None)
    return jax.shard_map(
        per_device, mesh=mesh, in_specs=in_specs, out_specs=out_specs, check_vma=False
    )
```
